512 devices in a mesh: dp: 16 (over z), expert: 32 (over y, x, core).
Axes of the slice: x: 4, y: 4, z: 16, core: 2. Of those that a mesh axis runs over, the one named last changes fastest.
Arguments:
- tokens: bfloat16 [4096, 4096], P('expert', 'dp'), may hold values from -6 to 6
- routing: int32 [4096, 8], P('expert'), may hold values from 0 to 31, all different within a row; in each aligned block of 128 rows (0 to 127, 128 to 255, ...) at most 40 rows name the same one
- gate_probs: float32 [4096, 8], P('expert'), may hold values from 0.05 to 0.3
- paired: int32 [32], P('expert'), may hold values from 0 to 1, as said below
- w_gate: bfloat16 [32, 4096, 768], P('expert', 'dp'), may hold values from -0.09375 to 0.09375
- w_up: bfloat16 [32, 4096, 768], P('expert', 'dp'), may hold values from -0.09375 to 0.09375
- w_down: bfloat16 [32, 768, 4096], P('expert', None, 'dp'), may hold values from -0.21875 to 0.21875
- cotangent: bfloat16 [4096, 4096], P('expert', 'dp'), may hold values from -6 to 6
Outputs:
- output: bfloat16 [4096, 4096], P('expert', 'dp')
- grad_tokens: bfloat16 [4096, 4096], P('expert', 'dp')
- grad_gate: float32 [32, 4096, 768], P('expert', 'dp')
- grad_up: float32 [32, 4096, 768], P('expert', 'dp')
- grad_down: float32 [32, 768, 4096], P('expert', None, 'dp')
The draws below stay inside these ranges and needn't reach their ends.
Inputs may be any that keep to these rules, and one draw needn't show every extreme that they name: `routing`: each token names 8 different copies; among the tokens of one source (aligned blocks of 128 tokens) no copy is named more than 40 times, a bound that some block reaches. paired[c] equals paired[(c + 16) mod 32]; paired[0] and paired[31] are 1.
All inputs are finite; a program needn't handle non-finite values.
Results may differ from the reference program's by a relative error of at most 0.029.
Values may be sent and summed in bfloat16 or wider, within the bound.
A program may use at most 64 MiB of HBM per device.

```python
import math
import jax
import jax.numpy as jnp
import numpy as np
from jax import lax

D = 4096
H = 768
TOPK = 8
TOK_DEV = 128
COPIES = 32
CAP = 40
TOKENS = 4096
N_DP = 16


def draw_paired(key, part):
    half = jax.random.randint(key, (COPIES // 2,), 0, 2).astype(jnp.int32)
    half = half.at[0].set(1)
    half = half.at[COPIES // 2 - 1].set(1)
    return jnp.concatenate([half, half]).astype(jnp.int32)


def level_of(key, dims, pieces, smallest, largest):
    factor_of, own = 1.0, jax.random.fold_in(key, 6)
    for dim, blocks in pieces:
        heights = jnp.exp(jax.random.uniform(jax.random.fold_in(own, dim), (blocks,), jnp.float32, smallest / len(pieces), largest / len(pieces)))
        factor_of = factor_of * jnp.repeat(heights, dims[dim] // blocks).reshape([-1 if axis == dim else 1 for axis in range(len(dims))])
    return factor_of


def routed_block(own_key, own, number, rows, number_of, top, bound, skew):
    sequence = jax.random.permutation(own_key, number_of)
    heavy_load, common = load_shares(number_of, rows * top, bound, skew, True), load_shares(number_of, rows * top, bound, skew, False)
    places = jnp.arange(number_of)

    def named(lengths, rotation):
        used = int((lengths > 0).sum())
        fixed = max(1, used // 4)
        shifted = fixed + (places - fixed + rotation * (used - fixed)) % max(1, number_of - fixed)
        return jnp.zeros((number_of,), jnp.int32).at[sequence[jnp.where(places < fixed, places, shifted)]].set(jnp.asarray(lengths, jnp.int32))

    lengths = jnp.where(number % 4 == 0, named(heavy_load, number // 4), named(common, number - number // 4 - 1))
    mixed = jax.random.permutation(jax.random.fold_in(own, 3), number_of)
    giver, taker = mixed[0:number_of // 2 * 2:2], mixed[1:number_of // 2 * 2:2]
    room = jnp.minimum(lengths[giver] - 1, bound - lengths[taker]) // 2
    room = jnp.where((giver == sequence[0]) | (taker == sequence[0]) | (lengths[taker] == 0), 0, jnp.maximum(room, 0))
    shifted = jax.random.randint(jax.random.fold_in(own, 4), (number_of // 2,), 0, 1 << 20) % (room + 1)
    lengths = lengths.at[giver].add(-shifted).at[taker].add(shifted)
    items = jnp.searchsorted(jnp.cumsum(lengths), jnp.arange(rows * top), side="right").astype(jnp.int32)
    table = items.reshape(top, rows).T
    table = table[jax.random.permutation(jax.random.fold_in(own, 1), rows)]
    rotation = jax.random.randint(jax.random.fold_in(own, 2), (rows, 1), 0, top)
    return jnp.take_along_axis(table, (jnp.arange(top)[None, :] + rotation) % top, axis=1)


def load_shares(amount, total, bound, lean, full):
    portions = [(1 << 20) // math.isqrt(grade ** lean) + 1 for grade in range(1, amount + 1)]
    largest = bound if full else min(bound, max(-(-total // amount), total * portions[0] // sum(portions)))
    least = 1 if total - largest >= amount - 1 else 0
    holding, surplus = [largest] + [least] * (amount - 1), total - largest - least * (amount - 1)
    while surplus > 0:
        movable = [i for i in range(1, amount) if holding[i] < largest] or [i for i in range(1, amount) if holding[i] < bound]
        pool, left = sum([portions[i] for i in movable]), surplus
        for i in movable:
            more = min(bound - holding[i], max(1, left * portions[i] // pool), surplus)
            holding[i] = holding[i] + more
            surplus = surplus - more
    return np.array(holding)


def normal_values(rng, dims, scale, most, cuts=(), kind=jnp.bfloat16):
    loudness = level_of(rng, dims, cuts, -0.22, 0.18) if cuts else 1.0
    result = jax.random.normal(rng, dims, jnp.float32) * scale * loudness
    return jnp.minimum(jnp.maximum(result, -most), most).astype(kind)


def setup_inputs(seed: int = 0) -> dict:
    seeds = jax.random.split(jax.random.key(seed), 9)
    tokens = normal_values(seeds[0], (TOKENS, D), 1.0, 6.0, ((0, 32), (1, 16)))
    routing_keys = jax.random.split(jax.random.fold_in(seeds[1], 1), TOKENS // TOK_DEV)
    routing_turns = jax.random.permutation(jax.random.fold_in(seeds[1], 3), TOKENS // TOK_DEV)
    routing = jax.vmap(lambda own, number: routed_block(jax.random.fold_in(seeds[1], 2), own, number, TOK_DEV, COPIES, TOPK, CAP, 1))(routing_keys, routing_turns).reshape((TOKENS, TOPK))
    gate_probs = jnp.clip(0.05 + 0.25 * jax.random.uniform(seeds[2], (TOKENS, TOPK), jnp.float32) ** level_of(seeds[2], (TOKENS, TOPK), ((0, 32),), -0.2, 0.2), 0.05, 0.3)
    paired = draw_paired(jax.random.fold_in(seeds[8], 71), 0)
    w_gate = normal_values(seeds[4], (COPIES, D, H), D ** -0.5, 0.09375, ((0, 32), (1, 16)))
    w_up = normal_values(seeds[5], (COPIES, D, H), D ** -0.5, 0.09375, ((0, 32), (1, 16)))
    w_down = normal_values(seeds[6], (COPIES, H, D), H ** -0.5, 0.21875, ((0, 32), (2, 16)))
    cotangent = normal_values(seeds[7], (TOKENS, D), 1.0, 6.0, ((0, 32), (1, 16)))
    return {"tokens": tokens, "routing": routing, "gate_probs": gate_probs, "paired": paired, "w_gate": w_gate, "w_up": w_up, "w_down": w_down, "cotangent": cotangent}


def rounded(value):
    return lax.optimization_barrier(value.astype(jnp.bfloat16)).astype(jnp.float32)


def expert_pass(rows_in, rows_grad, gate_weight, up_weight, down_weight):
    count = rows_in.shape[0]
    width = rows_in.shape[1]
    slab = width // N_DP
    hidden = gate_weight.shape[1]
    blocks_in = rows_in.reshape(count, N_DP, slab).astype(jnp.float32)
    blocks_grad = rows_grad.reshape(count, N_DP, slab).astype(jnp.float32)
    gate_blocks = gate_weight.reshape(N_DP, slab, hidden).astype(jnp.float32)
    up_blocks = up_weight.reshape(N_DP, slab, hidden).astype(jnp.float32)
    down_blocks = down_weight.reshape(hidden, N_DP, slab).astype(jnp.float32)
    gate = jnp.sum(rounded(jnp.einsum("rjd,jdh->jrh", blocks_in, gate_blocks)), axis=0)
    upper = jnp.sum(rounded(jnp.einsum("rjd,jdh->jrh", blocks_in, up_blocks)), axis=0)
    sigma = jax.nn.sigmoid(gate)
    activated = gate * sigma
    hid = (activated * upper).astype(jnp.bfloat16)
    out = jnp.dot(hid, down_weight, preferred_element_type=jnp.float32).astype(jnp.bfloat16)
    grad_down = jnp.dot(hid.T, rows_grad, preferred_element_type=jnp.float32)
    grad_hid = jnp.sum(rounded(jnp.einsum("rjd,hjd->jrh", blocks_grad, down_blocks)), axis=0)
    grad_gate_rows = (grad_hid * upper * sigma * (1.0 + gate * (1.0 - sigma))).astype(jnp.bfloat16)
    grad_up_rows = (grad_hid * activated).astype(jnp.bfloat16)
    grad_gate = jnp.dot(rows_in.T, grad_gate_rows, preferred_element_type=jnp.float32)
    grad_up = jnp.dot(rows_in.T, grad_up_rows, preferred_element_type=jnp.float32)
    back = jnp.dot(grad_gate_rows, gate_weight.T, preferred_element_type=jnp.float32)
    back = back + jnp.dot(grad_up_rows, up_weight.T, preferred_element_type=jnp.float32)
    return out, back.astype(jnp.bfloat16), grad_gate, grad_up, grad_down


def reference(tokens, routing, gate_probs, paired, w_gate, w_up, w_down, cotangent):
    token_total = routing.shape[0]
    top_count = routing.shape[1]
    width = tokens.shape[1]
    sources = token_total // TOK_DEV
    source_rows = TOK_DEV * top_count
    flat = routing.reshape(sources, source_rows)
    onehot = (flat[:, :, None] == jnp.arange(COPIES, dtype=jnp.int32)[None, None, :]).astype(jnp.int32)
    earlier = jnp.cumsum(onehot, axis=1) - onehot
    slot = jnp.sum(earlier * onehot, axis=2)
    position = (jnp.arange(sources, dtype=jnp.int32)[:, None] * CAP + slot).reshape(-1).astype(jnp.int32)
    copy_of = flat.reshape(-1).astype(jnp.int32)
    all_rows = token_total * top_count
    table = jnp.full((COPIES, sources * CAP), all_rows, dtype=jnp.int32)
    table = table.at[copy_of, position].set(jnp.arange(all_rows, dtype=jnp.int32))
    token_rows = jnp.concatenate([jnp.repeat(tokens, top_count, axis=0), jnp.zeros((1, width), tokens.dtype)], axis=0)
    scaled = (gate_probs[:, :, None] * cotangent.astype(jnp.float32)[:, None, :]).astype(jnp.bfloat16)
    grad_rows = jnp.concatenate([scaled.reshape(all_rows, width), jnp.zeros((1, width), jnp.bfloat16)], axis=0)

    def one_copy(packed):
        index, gate_weight, up_weight, down_weight = packed
        return expert_pass(token_rows[index], grad_rows[index], gate_weight, up_weight, down_weight)

    outs, backs, grad_gate, grad_up, grad_down = lax.map(one_copy, (table, w_gate, w_up, w_down))
    where = copy_of * (sources * CAP) + position
    out_rows = outs.reshape(-1, width)[where].reshape(token_total, top_count, width)
    back_rows = backs.reshape(-1, width)[where].reshape(token_total, top_count, width)
    output = jnp.sum(gate_probs[:, :, None] * out_rows.astype(jnp.float32), axis=1).astype(jnp.bfloat16)
    grad_tokens = jnp.sum(back_rows.astype(jnp.float32), axis=1).astype(jnp.bfloat16)
    partner = (jnp.arange(COPIES, dtype=jnp.int32) + COPIES // 2) % COPIES
    keep = paired.astype(jnp.float32)[:, None, None]
    grad_gate = grad_gate + keep * grad_gate[partner]
    grad_up = grad_up + keep * grad_up[partner]
    grad_down = grad_down + keep * grad_down[partner]
    return output, grad_tokens, grad_gate, grad_up, grad_down
```

```python
import functools

import jax
import jax.numpy as jnp
from jax import lax
from jax.experimental import pallas as pl
from jax.experimental.pallas import tpu as pltpu
from jax.sharding import PartitionSpec as P

F32 = jnp.float32
BF16 = jnp.bfloat16
MESH = pl.DeviceIdType.MESH


def nn(left, right):
    return jnp.dot(left, right, preferred_element_type=F32)


def tn(left, right):
    return lax.dot_general(left, right, (((0,), (0,)), ((), ())), preferred_element_type=F32)


def nt(left, right):
    return lax.dot_general(left, right, (((1,), (1,)), ((), ())), preferred_element_type=F32)


def layer(
    n,
    n_exp,
    cap,
    paired,
    route,
    prob,
    tokens,
    cotangent,
    wg,
    wu,
    wd,
    y,
    gt,
    gg,
    gu,
    gd,
    sel,
    high,
    low,
    row_prob,
    stage_x,
    stage_g,
    land_x,
    land_g,
    xb,
    gb,
    part_gu,
    part_d,
    land_gu,
    land_d,
    own_gu,
    act,
    stage_o,
    stage_b,
    home_o,
    home_b,
    pair_out,
    pair_in,
    x_s,
    x_r,
    g_s,
    g_r,
    o_s,
    o_r,
    b_s,
    b_r,
    local_s,
    rs_s,
    rs_r,
    ag_s,
    ag_r,
    pair_s,
    pair_r,
):
    top, count = route.shape
    width, hidden = wg.shape
    rows = n_exp * cap
    own = rows // n
    per = n_exp // n
    half = hidden // 2
    third = hidden // 3
    hops = n // 2
    z = lax.axis_index("dp")
    me = lax.axis_index("expert")
    group = me // per
    left = lax.rem(z + n - 1, n)
    right = lax.rem(z + 1, n)
    partner = lax.rem(me + n_exp // 2, n_exp)

    barrier = pltpu.get_barrier_semaphore()
    for neighbour in (left, right):
        pl.semaphore_signal(
            barrier, inc=1, device_id={"dp": neighbour}, device_id_type=MESH
        )

    @pl.loop(1, n_exp)
    def _(o):
        pl.semaphore_signal(
            barrier, inc=1, device_id={"expert": me ^ o}, device_id_type=MESH
        )

    def chunk(index):
        return pl.ds(pl.multiple_of(lax.rem(index + 4 * n, n) * own, own), own)

    def flat(value):
        return value.astype(F32).reshape(value.shape[0] * cap, width).astype(BF16)

    def blocks(value):
        return value.reshape(value.shape[0] // cap, cap, width).astype(BF16)

    def place(source, target):
        shift = lax.rem(source // per - target // per + n, n)
        return shift * per + lax.rem(source, per)

    copy_id = lax.broadcasted_iota(jnp.int32, (n_exp, count), 0)
    named = jnp.zeros((n_exp, count), F32)
    weight = jnp.zeros((n_exp, count), F32)
    for k in range(top):
        hit = copy_id == route[k : k + 1, :]
        named = named + jnp.where(hit, 1.0, 0.0)
        weight = weight + jnp.where(hit, prob[k : k + 1, :], 0.0)
    before = lax.broadcasted_iota(jnp.int32, (count, count), 0) < lax.broadcasted_iota(
        jnp.int32, (count, count), 1
    )
    earlier = nn(named.astype(BF16), jnp.where(before, 1.0, 0.0).astype(BF16))
    slot = jnp.where(named > 0.5, earlier, -1.0)
    place_id = lax.broadcasted_iota(jnp.int32, (cap, count), 0).astype(F32)
    for c in range(n_exp):
        hit = place_id == slot[c : c + 1, :]
        weighted = jnp.where(hit, weight[c : c + 1, :], 0.0)
        upper = weighted.astype(BF16)
        at = slice(c * cap, (c + 1) * cap)
        sel[at, :] = jnp.where(hit, 1.0, 0.0).astype(BF16)
        high[at, :] = upper
        low[at, :] = (weighted - upper.astype(F32)).astype(BF16)
        row_prob[at, :] = jnp.sum(weighted, axis=1, keepdims=True)

    parts = 4
    many = n_exp // parts
    size = rows // parts

    def dispatch_copy(stage, dest, send, recv, target):
        return pltpu.make_async_remote_copy(
            src_ref=stage.at[target],
            dst_ref=dest.at[place(me, target)],
            send_sem=send.at[me ^ target],
            recv_sem=recv.at[me ^ target],
            device_id={"expert": target},
            device_id_type=MESH,
        )

    def local_dispatch(stage, dest, index):
        return pltpu.make_async_copy(
            stage.at[me], dest.at[lax.rem(me, per)], local_s.at[index]
        )

    stage_x[...] = blocks(nn(sel[...], tokens[...]))
    pl.semaphore_wait(barrier, n_exp + 1)

    @pl.loop(1, n_exp)
    def _(o):
        dispatch_copy(stage_x, land_x, x_s, x_r, me ^ o).start()

    local_dispatch(stage_x, land_x, 0).start()
    stage_g[...] = blocks(nn(sel[...], cotangent[...]) * row_prob[...])

    @pl.loop(1, n_exp)
    def _(o):
        dispatch_copy(stage_g, land_g, g_s, g_r, me ^ o).start()

    local_dispatch(stage_g, land_g, 1).start()

    @pl.loop(1, n_exp)
    def _(o):
        dispatch_copy(stage_x, land_x, x_s, x_r, me ^ o).wait_recv()

    local_dispatch(stage_x, land_x, 0).wait()

    @pl.loop(0, parts)
    def _(b):
        at = pl.ds(pl.multiple_of(b * size, size), size)
        got = flat(land_x[pl.ds(b * many, many)])
        xb[at, :] = got
        part_gu[at, :hidden] = nn(got, wg[...]).astype(BF16)
        part_gu[at, hidden:] = nn(got, wu[...]).astype(BF16)

    streams = [
        (part_gu, 0, hidden, land_gu, 0),
        (part_gu, hidden, hidden, land_gu, 1),
        (part_d, 0, half, land_d, 0),
        (part_d, half, half, land_d, 1),
    ]
    started = []

    def reach(t, way):
        return hops if (t + way) % 2 == 0 else n - 1 - hops

    def rs_copy(t, way, s):
        part, col, wide, land, slab = streams[t]
        far = reach(t, way)
        dest = z + far - s if way == 0 else z - far + s
        src = part.at[chunk(dest), pl.ds(col, wide)] if s == 0 else land.at[slab, way, s - 1]
        return pltpu.make_async_remote_copy(
            src_ref=src,
            dst_ref=land.at[slab, way, s],
            send_sem=rs_s.at[t, way, s],
            recv_sem=rs_r.at[t, way, s],
            device_id={"dp": right if way == 0 else left},
            device_id_type=MESH,
        )

    def rs_send(t, way, s):
        if s < reach(t, way):
            copy = rs_copy(t, way, s)
            copy.start()
            started.append(copy)

    def rs_step(t, s):
        part, col, wide, land, slab = streams[t]
        for way in range(2):
            far = reach(t, way)
            if s < far:
                rs_copy(t, way, s).wait_recv()
                if s + 1 < far:
                    dest = z + far - 1 - s if way == 0 else z - far + 1 + s
                    mine = part[chunk(dest), col : col + wide].astype(F32)
                    land[slab, way, s] = (land[slab, way, s].astype(F32) + mine).astype(BF16)
                    rs_send(t, way, s + 1)

    def rs_total(t, col, wide):
        part, start, _, land, slab = streams[t]
        total = part[chunk(z), start + col : start + col + wide].astype(F32)
        for way in range(2):
            if reach(t, way):
                total = total + land[slab, way, reach(t, way) - 1, :, col : col + wide].astype(F32)
        return total

    def ag_copy(u, sub, way, s):
        at = z - s if way == 0 else z + s
        view = act.at[u, chunk(at), pl.ds(sub * half, half)]
        return pltpu.make_async_remote_copy(
            src_ref=view,
            dst_ref=view,
            send_sem=ag_s.at[u, sub, way, s],
            recv_sem=ag_r.at[u, sub, way, s],
            device_id={"dp": right if way == 0 else left},
            device_id_type=MESH,
        )

    def ag_recv(u, sub, way, s):
        at = z - 1 - s if way == 0 else z + 1 + s
        view = act.at[u, chunk(at), pl.ds(sub * half, half)]
        return pltpu.make_async_remote_copy(
            src_ref=view,
            dst_ref=view,
            send_sem=ag_s.at[u, sub, way, s],
            recv_sem=ag_r.at[u, sub, way, s],
            device_id={"dp": right if way == 0 else left},
            device_id_type=MESH,
        )

    def ag_send(u, sub, way, s):
        if s < reach(u + sub, way):
            copy = ag_copy(u, sub, way, s)
            copy.start()
            started.append(copy)

    def ag_first(u):
        for sub in range(2):
            for way in range(2):
                ag_send(u, sub, way, 0)

    def ag_step(u, s):
        for sub in range(2):
            for way in range(2):
                if s < reach(u + sub, way):
                    ag_recv(u, sub, way, s).wait_recv()
                    ag_send(u, sub, way, s + 1)

    def arrived(s):
        found = []
        for way in range(2):
            if s < n - 1 - hops:
                found.append(z - 1 - s if way == 0 else z + 1 + s)
        if s == hops - 1:
            found += [z + d for d in range(n - hops, hops + 1)]
        return found

    def home_copy(stage, home, send, recv, source, index):
        return pltpu.make_async_remote_copy(
            src_ref=stage.at[index],
            dst_ref=home.at[me],
            send_sem=send.at[me ^ source],
            recv_sem=recv.at[me ^ source],
            device_id={"expert": source},
            device_id_type=MESH,
        )

    def home_local(stage, home, index):
        return pltpu.make_async_copy(
            stage.at[lax.rem(me, per)], home.at[me], local_s.at[index]
        )

    def go_home(stage, home, send, recv, which, index):
        index = lax.rem(index + 4 * n, n)
        for sub in range(per):
            source = lax.rem(index + group, n) * per + sub

            @pl.when(source != me)
            def _():
                home_copy(stage, home, send, recv, source, index * per + sub).start()

            @pl.when(source == me)
            def _():
                home_local(stage, home, which).start()

    def answer(index):
        at = lax.rem(index + 4 * n, n) * per
        stage_o[pl.ds(at, per)] = blocks(nn(act[0, chunk(index), :], wd[...]))
        go_home(stage_o, home_o, o_s, o_r, 2, index)

    def back(index):
        at = lax.rem(index + 4 * n, n) * per
        stage_b[pl.ds(at, per)] = blocks(
            nt(act[1, chunk(index), :], wg[...]) + nt(act[2, chunk(index), :], wu[...])
        )
        go_home(stage_b, home_b, b_s, b_r, 3, index)

    def pair_copy(u, k):
        return pltpu.make_async_remote_copy(
            src_ref=pair_out.at[u, k],
            dst_ref=pair_in.at[u, k],
            send_sem=pair_s.at[u, k],
            recv_sem=pair_r.at[u, k],
            device_id={"expert": partner},
            device_id_type=MESH,
        )

    def weight_grad(u, k):
        cut = slice(k * third, (k + 1) * third)
        if u == 0:
            value = tn(act[0, :, cut], gb[...])
            gd[cut, :] = value
            pair_out[u, k] = value.astype(BF16)
        else:
            value = tn(xb[...], act[u, :, cut])
            (gg if u == 1 else gu)[:, cut] = value
            pair_out[u, k] = value.astype(BF16)
        pair_copy(u, k).start()

    for way in range(2):
        for t in range(2):
            rs_send(t, way, 0)

    @pl.loop(1, n_exp)
    def _(o):
        dispatch_copy(stage_g, land_g, g_s, g_r, me ^ o).wait_recv()

    local_dispatch(stage_g, land_g, 1).wait()

    for s in range(hops):
        for t in range(2):
            rs_step(t, s)
        if s == 0:

            @pl.loop(0, parts)
            def _(b):
                at = pl.ds(pl.multiple_of(b * size, size), size)
                got = flat(land_g[pl.ds(b * many, many)])
                gb[at, :] = got
                part_d[at, :] = nt(got, wd[...]).astype(BF16)

        if s == max(hops - 2, 0):
            for way in range(2):
                for t in range(2, 4):
                    rs_send(t, way, 0)

    step = 128 if half % 128 == 0 else half
    for col in range(0, hidden, step):
        gate = rs_total(0, col, step)
        up = rs_total(1, col, step)
        own_gu[:, col : col + step] = gate
        own_gu[:, hidden + col : hidden + col + step] = up
        act[0, chunk(z), col : col + step] = (gate * jax.nn.sigmoid(gate) * up).astype(BF16)
    ag_first(0)

    for s in range(hops):
        for t in range(2, 4):
            rs_step(t, s)
        if s >= 2:
            ag_step(0, s - 2)
            for index in arrived(s - 2):
                answer(index)
        if s == 1:
            answer(z)

    for col in range(0, hidden, step):
        gate = own_gu[:, col : col + step]
        up = own_gu[:, hidden + col : hidden + col + step]
        t = 2 if col < half else 3
        grad = rs_total(t, col % half, step)
        sigma = jax.nn.sigmoid(gate)
        act[1, chunk(z), col : col + step] = (
            grad * up * sigma * (1.0 + gate * (1.0 - sigma))
        ).astype(BF16)
        act[2, chunk(z), col : col + step] = (grad * (gate * sigma)).astype(BF16)
    ag_first(1)
    for s in range(max(hops - 2, 0), hops):
        ag_step(0, s)
        for index in arrived(s):
            answer(index)
    for s in range(hops):
        ag_step(1, s)
        if s < 3:
            weight_grad(0, s)
        if s == max(hops - 2, 0):
            ag_first(2)
    for k in range(hops, 3):
        weight_grad(0, k)
    back(z)
    for s in range(hops):
        ag_step(2, s)
        for index in arrived(s):
            back(index)
        if s < 3:
            weight_grad(1, s)
    for k in range(hops, 3):
        weight_grad(1, k)
    for k in range(3):
        weight_grad(2, k)

    @pl.loop(1, n_exp)
    def _(o):
        pltpu.make_async_remote_copy(
            src_ref=stage_o.at[place(me ^ o, me)],
            dst_ref=home_o.at[me ^ o],
            send_sem=o_s.at[o],
            recv_sem=o_r.at[o],
            device_id={"expert": me ^ o},
            device_id_type=MESH,
        ).wait()

    home_local(stage_o, home_o, 2).wait()
    got = flat(home_o[...])
    y[...] = (tn(high[...], got) + tn(low[...], got)).astype(BF16)

    @pl.loop(1, n_exp)
    def _(o):
        pltpu.make_async_remote_copy(
            src_ref=stage_b.at[place(me ^ o, me)],
            dst_ref=home_b.at[me ^ o],
            send_sem=b_s.at[o],
            recv_sem=b_r.at[o],
            device_id={"expert": me ^ o},
            device_id_type=MESH,
        ).wait()

    home_local(stage_b, home_b, 3).wait()
    gt[...] = tn(sel[...], flat(home_b[...])).astype(BF16)

    keep = paired[0].astype(F32)
    for u in range(3):
        for k in range(3):
            cut = slice(k * third, (k + 1) * third)
            pair_copy(u, k).wait()
            other = pair_in[u, k].astype(F32) * keep
            if u == 0:
                gd[cut, :] = gd[cut, :] + other
            elif u == 1:
                gg[:, cut] = gg[:, cut] + other
            else:
                gu[:, cut] = gu[:, cut] + other

    for copy in started:
        copy.wait_send()

    @pl.loop(1, n_exp)
    def _(o):
        dispatch_copy(stage_x, land_x, x_s, x_r, me ^ o).wait_send()
        dispatch_copy(stage_g, land_g, g_s, g_r, me ^ o).wait_send()


def per_device(tokens, routing, gate_probs, paired, w_gate, w_up, w_down, cotangent):
    n_exp = lax.axis_size("expert")
    n = lax.axis_size("dp")
    count, top = routing.shape
    width = tokens.shape[1]
    hidden = w_gate.shape[2]
    cap = max(2, 5 * count * top // (4 * n_exp))
    rows = n_exp * cap
    own = rows // n
    half = hidden // 2
    third = hidden // 3
    hops = n // 2
    vmem = pl.BlockSpec(memory_space=pltpu.VMEM)
    dma = pltpu.SemaphoreType.DMA
    outs = pl.pallas_call(
        functools.partial(layer, n, n_exp, cap),
        out_shape=(
            jax.ShapeDtypeStruct((count, width), BF16),
            jax.ShapeDtypeStruct((count, width), BF16),
            jax.ShapeDtypeStruct((width, hidden), F32),
            jax.ShapeDtypeStruct((width, hidden), F32),
            jax.ShapeDtypeStruct((hidden, width), F32),
        ),
        in_specs=[pl.BlockSpec(memory_space=pltpu.SMEM)] + [vmem] * 7,
        out_specs=(vmem,) * 5,
        scratch_shapes=[
            pltpu.VMEM((rows, count), BF16),
            pltpu.VMEM((rows, count), BF16),
            pltpu.VMEM((rows, count), BF16),
            pltpu.VMEM((rows, 1), F32),
            pltpu.VMEM((n_exp, cap, width), BF16),
            pltpu.VMEM((n_exp, cap, width), BF16),
            pltpu.VMEM((n_exp, cap, width), BF16),
            pltpu.VMEM((n_exp, cap, width), BF16),
            pltpu.VMEM((rows, width), BF16),
            pltpu.VMEM((rows, width), BF16),
            pltpu.VMEM((rows, 2 * hidden), BF16),
            pltpu.VMEM((rows, hidden), BF16),
            pltpu.VMEM((2, 2, hops, own, hidden), BF16),
            pltpu.VMEM((2, 2, hops, own, half), BF16),
            pltpu.VMEM((own, 2 * hidden), F32),
            pltpu.VMEM((3, rows, hidden), BF16),
            pltpu.VMEM((n_exp, cap, width), BF16),
            pltpu.VMEM((n_exp, cap, width), BF16),
            pltpu.VMEM((n_exp, cap, width), BF16),
            pltpu.VMEM((n_exp, cap, width), BF16),
            pltpu.VMEM((3, 3, third, width), BF16),
            pltpu.VMEM((3, 3, third, width), BF16),
            dma((n_exp,)),
            dma((n_exp,)),
            dma((n_exp,)),
            dma((n_exp,)),
            dma((n_exp,)),
            dma((n_exp,)),
            dma((n_exp,)),
            dma((n_exp,)),
            dma((4,)),
            dma((4, 2, hops)),
            dma((4, 2, hops)),
            dma((3, 2, 2, hops)),
            dma((3, 2, 2, hops)),
            dma((3, 3)),
            dma((3, 3)),
        ],
        compiler_params=pltpu.CompilerParams(
            collective_id=0, has_side_effects=True, vmem_limit_bytes=56 * 1024 * 1024
        ),
    )(
        paired,
        routing.T,
        gate_probs.T,
        tokens,
        cotangent,
        w_gate[0],
        w_up[0],
        w_down[0],
    )
    y, gt, gg, gu, gd = outs
    return y, gt, gg[None], gu[None], gd[None]


def solution(mesh):
    return jax.shard_map(
        per_device,
        mesh=mesh,
        in_specs=(
            P("expert", "dp"),
            P("expert", None),
            P("expert", None),
            P("expert"),
            P("expert", "dp", None),
            P("expert", "dp", None),
            P("expert", None, "dp"),
            P("expert", "dp"),
        ),
        out_specs=(
            P("expert", "dp"),
            P("expert", "dp"),
            P("expert", "dp", None),
            P("expert", "dp", None),
            P("expert", None, "dp"),
        ),
        check_vma=False,
    )
```

```python
import functools

import jax
import jax.numpy as jnp
from jax import lax
from jax.experimental import pallas as pl
from jax.experimental.pallas import tpu as pltpu
from jax.sharding import PartitionSpec as P

F32 = jnp.float32
BF16 = jnp.bfloat16
MESH = pl.DeviceIdType.MESH
LATE = 2


def nn(left, right):
    return jnp.dot(left, right, preferred_element_type=F32)


def tn(left, right):
    return lax.dot_general(left, right, (((0,), (0,)), ((), ())), preferred_element_type=F32)


def nt(left, right):
    return lax.dot_general(left, right, (((1,), (1,)), ((), ())), preferred_element_type=F32)


def layer(
    n,
    n_exp,
    cap,
    lag,
    late,
    route,
    prob,
    tokens,
    cotangent,
    wg_in,
    wu_in,
    wd_in,
    y,
    gt,
    grad_out,
    pair_got,
    wg,
    wu,
    wd,
    sel,
    high,
    low,
    row_prob,
    stage_x,
    stage_g,
    land_x,
    land_g,
    xb,
    gb,
    part_gu,
    part_d,
    land_gu,
    land_d,
    own_gu,
    act,
    stage_o,
    stage_b,
    home_o,
    home_b,
    grads,
    pair_out,
    pair_in,
    x_s,
    x_r,
    g_s,
    g_r,
    o_s,
    o_r,
    b_s,
    b_r,
    local_s,
    rs_s,
    rs_r,
    ag_s,
    ag_r,
    pair_s,
    pair_r,
    load_s,
    grad_s,
    got_s,
):
    top, count = route.shape
    width, hidden = wg_in.shape
    rows = n_exp * cap
    own = rows // n
    per = n_exp // n
    half = hidden // 2
    third = hidden // 3
    hops = n // 2
    z = lax.axis_index("dp")
    me = lax.axis_index("expert")
    group = me // per
    left = lax.rem(z + n - 1, n)
    right = lax.rem(z + 1, n)
    partner = lax.rem(me + n_exp // 2, n_exp)

    barrier = pltpu.get_barrier_semaphore()
    for neighbour in (left, right):
        pl.semaphore_signal(
            barrier, inc=1, device_id={"dp": neighbour}, device_id_type=MESH
        )

    @pl.loop(1, n_exp)
    def _(o):
        pl.semaphore_signal(
            barrier, inc=1, device_id={"expert": me ^ o}, device_id_type=MESH
        )

    loads = [
        pltpu.make_async_copy(src, dst, load_s.at[k])
        for k, (src, dst) in enumerate(((wg_in, wg), (wu_in, wu), (wd_in, wd)))
    ]
    for load in loads:
        load.start()

    def chunk(index):
        return pl.ds(pl.multiple_of(lax.rem(index + 4 * n, n) * own, own), own)

    def flat(value):
        return value.astype(F32).reshape(value.shape[0] * cap, width).astype(BF16)

    def blocks(value):
        return value.reshape(value.shape[0] // cap, cap, width).astype(BF16)

    def place(source, target):
        shift = lax.rem(source // per - target // per + n, n)
        return shift * per + lax.rem(source, per)

    copy_id = lax.broadcasted_iota(jnp.int32, (n_exp, count), 0)
    named = jnp.zeros((n_exp, count), F32)
    weight = jnp.zeros((n_exp, count), F32)
    for k in range(top):
        hit = copy_id == route[k : k + 1, :]
        named = named + jnp.where(hit, 1.0, 0.0)
        weight = weight + jnp.where(hit, prob[k : k + 1, :], 0.0)
    before = lax.broadcasted_iota(jnp.int32, (count, count), 0) < lax.broadcasted_iota(
        jnp.int32, (count, count), 1
    )
    earlier = nn(named.astype(BF16), jnp.where(before, 1.0, 0.0).astype(BF16))
    slot = jnp.where(named > 0.5, earlier, -1.0)
    place_id = lax.broadcasted_iota(jnp.int32, (cap, count), 0).astype(F32)
    for c in range(n_exp):
        hit = place_id == slot[c : c + 1, :]
        weighted = jnp.where(hit, weight[c : c + 1, :], 0.0)
        upper = weighted.astype(BF16)
        at = slice(c * cap, (c + 1) * cap)
        sel[at, :] = jnp.where(hit, 1.0, 0.0).astype(BF16)
        high[at, :] = upper
        low[at, :] = (weighted - upper.astype(F32)).astype(BF16)
        row_prob[at, :] = jnp.sum(weighted, axis=1, keepdims=True)

    order = [hops, hops - 1, 1 - hops]
    later = []
    for s in range(hops - 1):
        near = hops - 2 - s
        later.append([near, -near] if near else [0])
        order += later[-1]
    later += [[]] * (hops - len(later))

    def dispatch_copy(stage, dest, send, recv, target, source):
        return pltpu.make_async_remote_copy(
            src_ref=stage.at[target],
            dst_ref=dest.at[place(source, target)],
            send_sem=send.at[source ^ target],
            recv_sem=recv.at[source ^ target],
            device_id={"expert": target if source is me else source},
            device_id_type=MESH,
        )

    def local_dispatch(stage, dest, index):
        return pltpu.make_async_copy(
            stage.at[me], dest.at[lax.rem(me, per)], local_s.at[index]
        )

    def dispatch(stage, dest, send, recv, which, offsets):
        for offset in offsets:
            for sub in range(per):
                target = lax.rem(group - z - offset + 4 * n, n) * per + sub

                @pl.when(target != me)
                def _():
                    dispatch_copy(stage, dest, send, recv, target, me).start()

                @pl.when(target == me)
                def _():
                    local_dispatch(stage, dest, which).start()

    def await_chunk(stage, dest, send, recv, which, index):
        for sub in range(per):
            source = lax.rem(index + group + 4 * n, n) * per + sub

            @pl.when(source != me)
            def _():
                dispatch_copy(stage, dest, send, recv, me, source).wait_recv()

            @pl.when(source == me)
            def _():
                local_dispatch(stage, dest, which).wait()

    def fill_x(index):
        await_chunk(stage_x, land_x, x_s, x_r, 0, index)
        got = flat(land_x[pl.ds(lax.rem(index + 4 * n, n) * per, per)])
        xb[chunk(index), :] = got
        part_gu[chunk(index), :hidden] = nn(got, wg[...]).astype(BF16)
        part_gu[chunk(index), hidden:] = nn(got, wu[...]).astype(BF16)

    def fill_g(index):
        await_chunk(stage_g, land_g, g_s, g_r, 1, index)
        got = flat(land_g[pl.ds(lax.rem(index + 4 * n, n) * per, per)])
        gb[chunk(index), :] = got
        part_d[chunk(index), :] = nt(got, wd[...]).astype(BF16)

    stage_x[...] = blocks(nn(sel[...], tokens[...]))
    pl.semaphore_wait(barrier, n_exp + 1)
    dispatch(stage_x, land_x, x_s, x_r, 0, order)
    stage_g[...] = blocks(nn(sel[...], cotangent[...]) * row_prob[...])
    for load in loads:
        load.wait()
    for offset in order[:3]:
        fill_x(z + offset)

    streams = [
        (part_gu, 0, hidden, land_gu, 0),
        (part_gu, hidden, hidden, land_gu, 1),
        (part_d, 0, half, land_d, 0),
        (part_d, half, half, land_d, 1),
    ]
    started = []

    def reach(t, way):
        return hops if (t + way) % 2 == 0 else n - 1 - hops

    def rs_copy(t, way, s):
        part, col, wide, land, slab = streams[t]
        far = reach(t, way)
        dest = z + far - s if way == 0 else z - far + s
        src = part.at[chunk(dest), pl.ds(col, wide)] if s == 0 else land.at[slab, way, s - 1]
        return pltpu.make_async_remote_copy(
            src_ref=src,
            dst_ref=land.at[slab, way, s],
            send_sem=rs_s.at[t, way, s],
            recv_sem=rs_r.at[t, way, s],
            device_id={"dp": right if way == 0 else left},
            device_id_type=MESH,
        )

    def rs_send(t, way, s):
        if s < reach(t, way):
            copy = rs_copy(t, way, s)
            copy.start()
            started.append(copy)

    def rs_step(t, s):
        part, col, wide, land, slab = streams[t]
        for way in range(2):
            far = reach(t, way)
            if s < far:
                rs_copy(t, way, s).wait_recv()
                if s + 1 < far:
                    dest = z + far - 1 - s if way == 0 else z - far + 1 + s
                    mine = part[chunk(dest), col : col + wide].astype(F32)
                    land[slab, way, s] = (land[slab, way, s].astype(F32) + mine).astype(BF16)
                    rs_send(t, way, s + 1)

    def rs_total(t, col, wide):
        part, start, _, land, slab = streams[t]
        total = part[chunk(z), start + col : start + col + wide].astype(F32)
        for way in range(2):
            if reach(t, way):
                total = total + land[slab, way, reach(t, way) - 1, :, col : col + wide].astype(F32)
        return total

    def ag_copy(u, sub, way, s):
        at = z - s if way == 0 else z + s
        view = act.at[u, chunk(at), pl.ds(sub * half, half)]
        return pltpu.make_async_remote_copy(
            src_ref=view,
            dst_ref=view,
            send_sem=ag_s.at[u, sub, way, s],
            recv_sem=ag_r.at[u, sub, way, s],
            device_id={"dp": right if way == 0 else left},
            device_id_type=MESH,
        )

    def ag_recv(u, sub, way, s):
        at = z - 1 - s if way == 0 else z + 1 + s
        view = act.at[u, chunk(at), pl.ds(sub * half, half)]
        return pltpu.make_async_remote_copy(
            src_ref=view,
            dst_ref=view,
            send_sem=ag_s.at[u, sub, way, s],
            recv_sem=ag_r.at[u, sub, way, s],
            device_id={"dp": right if way == 0 else left},
            device_id_type=MESH,
        )

    def ag_send(u, sub, way, s):
        if s < reach(u + sub, way):
            copy = ag_copy(u, sub, way, s)
            copy.start()
            started.append(copy)

    def ag_first(u):
        for sub in range(2):
            for way in range(2):
                ag_send(u, sub, way, 0)

    def ag_step(u, s):
        for sub in range(2):
            for way in range(2):
                if s < reach(u + sub, way):
                    ag_recv(u, sub, way, s).wait_recv()
                    ag_send(u, sub, way, s + 1)

    def arrived(s):
        found = []
        for way in range(2):
            if s < n - 1 - hops:
                found.append(z - 1 - s if way == 0 else z + 1 + s)
        if s == hops - 1:
            found += [z + d for d in range(n - hops, hops + 1)]
        return found

    def home_copy(stage, home, send, recv, source, index):
        return pltpu.make_async_remote_copy(
            src_ref=stage.at[index],
            dst_ref=home.at[me],
            send_sem=send.at[me ^ source],
            recv_sem=recv.at[me ^ source],
            device_id={"expert": source},
            device_id_type=MESH,
        )

    def home_local(stage, home, index):
        return pltpu.make_async_copy(
            stage.at[lax.rem(me, per)], home.at[me], local_s.at[index]
        )

    def go_home(stage, home, send, recv, which, index):
        index = lax.rem(index + 4 * n, n)
        for sub in range(per):
            source = lax.rem(index + group, n) * per + sub

            @pl.when(source != me)
            def _():
                home_copy(stage, home, send, recv, source, index * per + sub).start()

            @pl.when(source == me)
            def _():
                home_local(stage, home, which).start()

    def answer(index):
        at = lax.rem(index + 4 * n, n) * per
        stage_o[pl.ds(at, per)] = blocks(nn(act[0, chunk(index), :], wd[...]))
        go_home(stage_o, home_o, o_s, o_r, 2, index)

    def back(index):
        at = lax.rem(index + 4 * n, n) * per
        stage_b[pl.ds(at, per)] = blocks(
            nt(act[1, chunk(index), :], wg[...]) + nt(act[2, chunk(index), :], wu[...])
        )
        go_home(stage_b, home_b, b_s, b_r, 3, index)

    def pair_copy(u, k):
        return pltpu.make_async_remote_copy(
            src_ref=pair_out.at[u, k],
            dst_ref=pair_in.at[u, k],
            send_sem=pair_s.at[u, k],
            recv_sem=pair_r.at[u, k],
            device_id={"expert": partner},
            device_id_type=MESH,
        )

    def grad_copy(u, k):
        piece = slice(k * third, (k + 1) * third)
        dest = grad_out[u].at[piece, :] if u == 0 else grad_out[u].at[:, piece]
        return pltpu.make_async_copy(grads.at[u, k], dest, grad_s.at[u, k])

    def got_copy(u, k):
        return pltpu.make_async_copy(pair_in.at[u, k], pair_got.at[u, k], got_s.at[u, k])

    def weight_grad(u, k):
        piece = slice(k * third, (k + 1) * third)
        if u == 0:
            value = tn(act[0, :, piece], gb[...])
        else:
            value = tn(xb[...], act[u, :, piece])
        pair_out[u, k] = value.astype(BF16)
        pair_copy(u, k).start()
        grads[u, k] = value
        grad_copy(u, k).start()

    step = 128 if half % 128 == 0 else half

    def activate():
        for col in range(0, hidden, step):
            gate = rs_total(0, col, step)
            up = rs_total(1, col, step)
            own_gu[:, col : col + step] = gate
            own_gu[:, hidden + col : hidden + col + step] = up
            act[0, chunk(z), col : col + step] = (gate * jax.nn.sigmoid(gate) * up).astype(BF16)

    def activate_grads():
        for col in range(0, hidden, step):
            gate = own_gu[:, col : col + step]
            up = own_gu[:, hidden + col : hidden + col + step]
            t = 2 if col < half else 3
            grad = rs_total(t, col % half, step)
            sigma = jax.nn.sigmoid(gate)
            act[1, chunk(z), col : col + step] = (
                grad * up * sigma * (1.0 + gate * (1.0 - sigma))
            ).astype(BF16)
            act[2, chunk(z), col : col + step] = (grad * (gate * sigma)).astype(BF16)

    for way in range(2):
        for t in range(2):
            rs_send(t, way, 0)

    first_d, first_hid = lag, hops
    first_gate = lag + hops
    first_up = first_gate + late
    pending = []
    for slot_id in range(first_up + hops):
        if slot_id < hops:
            for offset in later[slot_id]:
                fill_x(z + offset)
            for t in range(2):
                rs_step(t, slot_id)
                cut = 2 * slot_id + t
                if slot_id < first_d:
                    ahead = order[cut * n // (2 * first_d) : (cut + 1) * n // (2 * first_d)]
                    dispatch(stage_g, land_g, g_s, g_r, 1, ahead)
        s = slot_id - first_d
        if 0 <= s < hops:
            for offset in later[s]:
                fill_g(z + offset)
            for t in range(2, 4):
                rs_step(t, s)
        s = slot_id - first_hid
        if 0 <= s < hops:
            ag_step(0, s)
            for index in arrived(s):
                answer(index)
            if s == hops - 1:
                pending += [(0, k) for k in range(3)]
        s = slot_id - first_gate
        if 0 <= s < hops:
            ag_step(1, s)
            if s == hops - 1:
                pending += [(1, k) for k in range(3)]
        s = slot_id - first_up
        if 0 <= s < hops:
            ag_step(2, s)
            for index in arrived(s):
                back(index)
        if slot_id + 1 == first_d:
            for offset in order[:3]:
                fill_g(z + offset)
            for way in range(2):
                for t in range(2, 4):
                    rs_send(t, way, 0)
        if slot_id + 1 == first_hid:
            activate()
            ag_first(0)
            answer(z)
        if slot_id + 1 == first_gate:
            activate_grads()
            ag_first(1)
        if slot_id + 1 == first_up:
            ag_first(2)
            back(z)
        for item in pending:
            weight_grad(*item)
        pending = []
    for k in range(3):
        weight_grad(2, k)

    @pl.loop(1, n_exp)
    def _(o):
        pltpu.make_async_remote_copy(
            src_ref=stage_o.at[place(me ^ o, me)],
            dst_ref=home_o.at[me ^ o],
            send_sem=o_s.at[o],
            recv_sem=o_r.at[o],
            device_id={"expert": me ^ o},
            device_id_type=MESH,
        ).wait()

    home_local(stage_o, home_o, 2).wait()
    got = flat(home_o[...])
    y[...] = (tn(high[...], got) + tn(low[...], got)).astype(BF16)

    @pl.loop(1, n_exp)
    def _(o):
        pltpu.make_async_remote_copy(
            src_ref=stage_b.at[place(me ^ o, me)],
            dst_ref=home_b.at[me ^ o],
            send_sem=b_s.at[o],
            recv_sem=b_r.at[o],
            device_id={"expert": me ^ o},
            device_id_type=MESH,
        ).wait()

    home_local(stage_b, home_b, 3).wait()
    gt[...] = tn(sel[...], flat(home_b[...])).astype(BF16)

    for u in range(3):
        for k in range(3):
            pair_copy(u, k).wait()
            got_copy(u, k).start()
    for u in range(3):
        for k in range(3):
            grad_copy(u, k).wait()
            got_copy(u, k).wait()

    for copy in started:
        copy.wait_send()

    @pl.loop(1, n_exp)
    def _(o):
        dispatch_copy(stage_x, land_x, x_s, x_r, me ^ o, me).wait_send()
        dispatch_copy(stage_g, land_g, g_s, g_r, me ^ o, me).wait_send()


def finish(paired, y_in, gt_in, gd_in, gg_in, gu_in, other, y, gt, gd, gg, gu, mine, got, s_pass, s_mine, s_got, s_out):
    third = other.shape[2]
    keep = paired[...].astype(F32)
    moves = [
        pltpu.make_async_copy(y_in, y, s_pass.at[0]),
        pltpu.make_async_copy(gt_in, gt, s_pass.at[1]),
    ]

    def part(ref, u, k):
        piece = slice(k * third, (k + 1) * third)
        return ref.at[piece, :] if u == 0 else ref.at[:, piece]

    pieces = [(u, k) for u in range(3) for k in range(3)]
    ins, outs = (gd_in, gg_in, gu_in), (gd, gg, gu)
    loads = {}
    for u, k in pieces:
        loads[u, k] = (
            pltpu.make_async_copy(part(ins[u], u, k), mine.at[u, k], s_mine.at[u, k]),
            pltpu.make_async_copy(other.at[u, k], got.at[u, k], s_got.at[u, k]),
        )
        for load in loads[u, k]:
            load.start()
    for move in moves:
        move.start()
    for u, k in pieces:
        for load in loads[u, k]:
            load.wait()
        mine[u, k] = mine[u, k] + keep * got[u, k].astype(F32)
        move = pltpu.make_async_copy(mine.at[u, k], part(outs[u], u, k), s_out.at[u, k])
        move.start()
        moves.append(move)
    for move in moves:
        move.wait()


def layer_call(sizes, *refs):
    refs = list(refs)
    layer(*sizes, *refs[:9], tuple(refs[9:12]), *refs[12:])


def per_device(tokens, routing, gate_probs, paired, w_gate, w_up, w_down, cotangent):
    n_exp = lax.axis_size("expert")
    n = lax.axis_size("dp")
    count, top = routing.shape
    width = tokens.shape[1]
    hidden = w_gate.shape[2]
    cap = max(2, 5 * count * top // (4 * n_exp))
    rows = n_exp * cap
    own = rows // n
    half = hidden // 2
    third = hidden // 3
    hops = n // 2
    vmem = pl.BlockSpec(memory_space=pltpu.VMEM)
    hbm = pl.BlockSpec(memory_space=pl.ANY)
    dma = pltpu.SemaphoreType.DMA
    lag = min(4, max(hops - 1, 1))
    outs = pl.pallas_call(
        functools.partial(layer_call, (n, n_exp, cap, lag, LATE)),
        out_shape=(
            jax.ShapeDtypeStruct((count, width), BF16),
            jax.ShapeDtypeStruct((count, width), BF16),
            jax.ShapeDtypeStruct((hidden, width), F32),
            jax.ShapeDtypeStruct((width, hidden), F32),
            jax.ShapeDtypeStruct((width, hidden), F32),
            jax.ShapeDtypeStruct((3, 3, third, width), BF16),
        ),
        in_specs=[vmem] * 4 + [hbm] * 3,
        out_specs=(vmem, vmem, hbm, hbm, hbm, hbm),
        scratch_shapes=[
            pltpu.VMEM((width, hidden), BF16),
            pltpu.VMEM((width, hidden), BF16),
            pltpu.VMEM((hidden, width), BF16),
            pltpu.VMEM((rows, count), BF16),
            pltpu.VMEM((rows, count), BF16),
            pltpu.VMEM((rows, count), BF16),
            pltpu.VMEM((rows, 1), F32),
            pltpu.VMEM((n_exp, cap, width), BF16),
            pltpu.VMEM((n_exp, cap, width), BF16),
            pltpu.VMEM((n_exp, cap, width), BF16),
            pltpu.VMEM((n_exp, cap, width), BF16),
            pltpu.VMEM((rows, width), BF16),
            pltpu.VMEM((rows, width), BF16),
            pltpu.VMEM((rows, 2 * hidden), BF16),
            pltpu.VMEM((rows, hidden), BF16),
            pltpu.VMEM((2, 2, hops, own, hidden), BF16),
            pltpu.VMEM((2, 2, hops, own, half), BF16),
            pltpu.VMEM((own, 2 * hidden), F32),
            pltpu.VMEM((3, rows, hidden), BF16),
            pltpu.VMEM((n_exp, cap, width), BF16),
            pltpu.VMEM((n_exp, cap, width), BF16),
            pltpu.VMEM((n_exp, cap, width), BF16),
            pltpu.VMEM((n_exp, cap, width), BF16),
            pltpu.VMEM((3, 3, third, width), F32),
            pltpu.VMEM((3, 3, third, width), BF16),
            pltpu.VMEM((3, 3, third, width), BF16),
            dma((n_exp,)),
            dma((n_exp,)),
            dma((n_exp,)),
            dma((n_exp,)),
            dma((n_exp,)),
            dma((n_exp,)),
            dma((n_exp,)),
            dma((n_exp,)),
            dma((4,)),
            dma((4, 2, hops)),
            dma((4, 2, hops)),
            dma((3, 2, 2, hops)),
            dma((3, 2, 2, hops)),
            dma((3, 3)),
            dma((3, 3)),
            dma((3,)),
            dma((3, 3)),
            dma((3, 3)),
        ],
        compiler_params=pltpu.CompilerParams(
            collective_id=0, has_side_effects=True, vmem_limit_bytes=56 * 1024 * 1024
        ),
    )(
        routing.T,
        gate_probs.T,
        tokens,
        cotangent,
        w_gate[0],
        w_up[0],
        w_down[0],
    )
    y, gt, gd, gg, gu = pl.pallas_call(
        finish,
        out_shape=(
            jax.ShapeDtypeStruct((count, width), BF16),
            jax.ShapeDtypeStruct((count, width), BF16),
            jax.ShapeDtypeStruct((hidden, width), F32),
            jax.ShapeDtypeStruct((width, hidden), F32),
            jax.ShapeDtypeStruct((width, hidden), F32),
        ),
        in_specs=[vmem] + [hbm] * 6,
        out_specs=(hbm,) * 5,
        scratch_shapes=[
            pltpu.VMEM((3, 3, third, width), F32),
            pltpu.VMEM((3, 3, third, width), BF16),
            dma((2,)),
            dma((3, 3)),
            dma((3, 3)),
            dma((3, 3)),
        ],
        compiler_params=pltpu.CompilerParams(vmem_limit_bytes=58 * 1024 * 1024),
    )(paired.reshape(1, 1), *outs)
    return y, gt, gg[None], gu[None], gd[None]


def solution(mesh):
    return jax.shard_map(
        per_device,
        mesh=mesh,
        in_specs=(
            P("expert", "dp"),
            P("expert", None),
            P("expert", None),
            P("expert"),
            P("expert", "dp", None),
            P("expert", "dp", None),
            P("expert", None, "dp"),
            P("expert", "dp"),
        ),
        out_specs=(
            P("expert", "dp"),
            P("expert", "dp"),
            P("expert", "dp", None),
            P("expert", "dp", None),
            P("expert", None, "dp"),
        ),
        check_vma=False,
    )
```

```python
import functools

import jax
import jax.numpy as jnp
from jax import lax
from jax.experimental import pallas as pl
from jax.experimental.pallas import tpu as pltpu
from jax.sharding import PartitionSpec as P

F32 = jnp.float32
BF16 = jnp.bfloat16
MESH = pl.DeviceIdType.MESH
LATE = 4


def nn(left, right):
    return jnp.dot(left, right, preferred_element_type=F32)


def tn(left, right):
    return lax.dot_general(left, right, (((0,), (0,)), ((), ())), preferred_element_type=F32)


def nt(left, right):
    return lax.dot_general(left, right, (((1,), (1,)), ((), ())), preferred_element_type=F32)


def layer(
    n,
    n_exp,
    cap,
    lag,
    late,
    route,
    prob,
    tokens,
    cotangent,
    wg_in,
    wu_in,
    wd_in,
    y,
    gt,
    grad_out,
    pair_got,
    wg,
    wu,
    wd,
    sel,
    high,
    low,
    row_prob,
    stage_x,
    stage_g,
    land_x,
    land_g,
    xb,
    gb,
    part_gu,
    part_d,
    land_gu,
    land_d,
    own_gu,
    act,
    stage_o,
    stage_b,
    home_o,
    home_b,
    grads,
    pair_out,
    pair_in,
    x_s,
    x_r,
    g_s,
    g_r,
    o_s,
    o_r,
    b_s,
    b_r,
    local_s,
    rs_s,
    rs_r,
    ag_s,
    ag_r,
    pair_s,
    pair_r,
    load_s,
    grad_s,
    got_s,
):
    top, count = route.shape
    width, hidden = wg_in.shape
    rows = n_exp * cap
    own = rows // n
    per = n_exp // n
    half = hidden // 2
    third = hidden // 3
    hops = n // 2
    z = lax.axis_index("dp")
    me = lax.axis_index("expert")
    group = me // per
    left = lax.rem(z + n - 1, n)
    right = lax.rem(z + 1, n)
    partner = lax.rem(me + n_exp // 2, n_exp)

    barrier = pltpu.get_barrier_semaphore()
    for neighbour in (left, right):
        pl.semaphore_signal(
            barrier, inc=1, device_id={"dp": neighbour}, device_id_type=MESH
        )

    @pl.loop(1, n_exp)
    def _(o):
        pl.semaphore_signal(
            barrier, inc=1, device_id={"expert": me ^ o}, device_id_type=MESH
        )

    loads = [
        pltpu.make_async_copy(src, dst, load_s.at[k])
        for k, (src, dst) in enumerate(((wg_in, wg), (wu_in, wu), (wd_in, wd)))
    ]
    for load in loads:
        load.start()

    def chunk(index):
        return pl.ds(pl.multiple_of(lax.rem(index + 4 * n, n) * own, own), own)

    def flat(value):
        return value.astype(F32).reshape(value.shape[0] * cap, width).astype(BF16)

    def blocks(value):
        return value.reshape(value.shape[0] // cap, cap, width).astype(BF16)

    def place(source, target):
        shift = lax.rem(source // per - target // per + n, n)
        return shift * per + lax.rem(source, per)

    copy_id = lax.broadcasted_iota(jnp.int32, (n_exp, count), 0)
    named = jnp.zeros((n_exp, count), F32)
    weight = jnp.zeros((n_exp, count), F32)
    for k in range(top):
        hit = copy_id == route[k : k + 1, :]
        named = named + jnp.where(hit, 1.0, 0.0)
        weight = weight + jnp.where(hit, prob[k : k + 1, :], 0.0)
    before = lax.broadcasted_iota(jnp.int32, (count, count), 0) < lax.broadcasted_iota(
        jnp.int32, (count, count), 1
    )
    earlier = nn(named.astype(BF16), jnp.where(before, 1.0, 0.0).astype(BF16))
    slot = jnp.where(named > 0.5, earlier, -1.0)
    place_id = lax.broadcasted_iota(jnp.int32, (cap, count), 0).astype(F32)
    for c in range(n_exp):
        hit = place_id == slot[c : c + 1, :]
        weighted = jnp.where(hit, weight[c : c + 1, :], 0.0)
        upper = weighted.astype(BF16)
        at = slice(c * cap, (c + 1) * cap)
        sel[at, :] = jnp.where(hit, 1.0, 0.0).astype(BF16)
        high[at, :] = upper
        low[at, :] = (weighted - upper.astype(F32)).astype(BF16)
        row_prob[at, :] = jnp.sum(weighted, axis=1, keepdims=True)

    order = [hops, hops - 1, 1 - hops]
    later = []
    for s in range(hops - 1):
        near = hops - 2 - s
        later.append([near, -near] if near else [0])
        order += later[-1]
    later += [[]] * (hops - len(later))

    def dispatch_copy(stage, dest, send, recv, target, source):
        return pltpu.make_async_remote_copy(
            src_ref=stage.at[target],
            dst_ref=dest.at[place(source, target)],
            send_sem=send.at[source ^ target],
            recv_sem=recv.at[source ^ target],
            device_id={"expert": target if source is me else source},
            device_id_type=MESH,
        )

    def local_dispatch(stage, dest, index):
        return pltpu.make_async_copy(
            stage.at[me], dest.at[lax.rem(me, per)], local_s.at[index]
        )

    def dispatch(stage, dest, send, recv, which, offsets):
        for offset in offsets:
            for sub in range(per):
                target = lax.rem(group - z - offset + 4 * n, n) * per + sub

                @pl.when(target != me)
                def _():
                    dispatch_copy(stage, dest, send, recv, target, me).start()

                @pl.when(target == me)
                def _():
                    local_dispatch(stage, dest, which).start()

    def await_chunk(stage, dest, send, recv, which, index):
        for sub in range(per):
            source = lax.rem(index + group + 4 * n, n) * per + sub

            @pl.when(source != me)
            def _():
                dispatch_copy(stage, dest, send, recv, me, source).wait_recv()

            @pl.when(source == me)
            def _():
                local_dispatch(stage, dest, which).wait()

    def fill_x(index):
        await_chunk(stage_x, land_x, x_s, x_r, 0, index)
        got = flat(land_x[pl.ds(lax.rem(index + 4 * n, n) * per, per)])
        xb[chunk(index), :] = got
        part_gu[chunk(index), :hidden] = nn(got, wg[...]).astype(BF16)
        part_gu[chunk(index), hidden:] = nn(got, wu[...]).astype(BF16)

    def fill_g(index):
        await_chunk(stage_g, land_g, g_s, g_r, 1, index)
        got = flat(land_g[pl.ds(lax.rem(index + 4 * n, n) * per, per)])
        gb[chunk(index), :] = got
        part_d[chunk(index), :] = nt(got, wd[...]).astype(BF16)

    stage_x[...] = blocks(nn(sel[...], tokens[...]))
    pl.semaphore_wait(barrier, n_exp + 1)
    dispatch(stage_x, land_x, x_s, x_r, 0, order)
    stage_g[...] = blocks(nn(sel[...], cotangent[...]) * row_prob[...])
    for load in loads:
        load.wait()
    for offset in order[:3]:
        fill_x(z + offset)

    streams = [
        (part_gu, 0, hidden, land_gu, 0),
        (part_gu, hidden, hidden, land_gu, 1),
        (part_d, 0, half, land_d, 0),
        (part_d, half, half, land_d, 1),
    ]
    started = []

    def reach(t, way):
        return hops if (t + way) % 2 == 0 else n - 1 - hops

    def rs_copy(t, way, s):
        part, col, wide, land, slab = streams[t]
        far = reach(t, way)
        dest = z + far - s if way == 0 else z - far + s
        src = part.at[chunk(dest), pl.ds(col, wide)] if s == 0 else land.at[slab, way, s - 1]
        return pltpu.make_async_remote_copy(
            src_ref=src,
            dst_ref=land.at[slab, way, s],
            send_sem=rs_s.at[t, way, s],
            recv_sem=rs_r.at[t, way, s],
            device_id={"dp": right if way == 0 else left},
            device_id_type=MESH,
        )

    def rs_send(t, way, s):
        if s < reach(t, way):
            copy = rs_copy(t, way, s)
            copy.start()
            started.append(copy)

    def rs_step(t, s):
        part, col, wide, land, slab = streams[t]
        for way in range(2):
            far = reach(t, way)
            if s < far:
                rs_copy(t, way, s).wait_recv()
                if s + 1 < far:
                    dest = z + far - 1 - s if way == 0 else z - far + 1 + s
                    mine = part[chunk(dest), col : col + wide].astype(F32)
                    land[slab, way, s] = (land[slab, way, s].astype(F32) + mine).astype(BF16)
                    rs_send(t, way, s + 1)

    def rs_total(t, col, wide):
        part, start, _, land, slab = streams[t]
        total = part[chunk(z), start + col : start + col + wide].astype(F32)
        for way in range(2):
            if reach(t, way):
                total = total + land[slab, way, reach(t, way) - 1, :, col : col + wide].astype(F32)
        return total

    def ag_copy(u, sub, way, s):
        at = z - s if way == 0 else z + s
        view = act.at[u, chunk(at), pl.ds(sub * half, half)]
        return pltpu.make_async_remote_copy(
            src_ref=view,
            dst_ref=view,
            send_sem=ag_s.at[u, sub, way, s],
            recv_sem=ag_r.at[u, sub, way, s],
            device_id={"dp": right if way == 0 else left},
            device_id_type=MESH,
        )

    def ag_recv(u, sub, way, s):
        at = z - 1 - s if way == 0 else z + 1 + s
        view = act.at[u, chunk(at), pl.ds(sub * half, half)]
        return pltpu.make_async_remote_copy(
            src_ref=view,
            dst_ref=view,
            send_sem=ag_s.at[u, sub, way, s],
            recv_sem=ag_r.at[u, sub, way, s],
            device_id={"dp": right if way == 0 else left},
            device_id_type=MESH,
        )

    def ag_send(u, sub, way, s):
        if s < reach(u + sub, way):
            copy = ag_copy(u, sub, way, s)
            copy.start()
            started.append(copy)

    def ag_first(u, sub):
        for way in range(2):
            ag_send(u, sub, way, 0)

    def ag_step(u, s):
        for sub in range(2):
            for way in range(2):
                if s < reach(u + sub, way):
                    ag_recv(u, sub, way, s).wait_recv()
                    ag_send(u, sub, way, s + 1)

    def arrived(s):
        found = []
        for way in range(2):
            if s < n - 1 - hops:
                found.append(z - 1 - s if way == 0 else z + 1 + s)
        if s == hops - 1:
            found += [z + d for d in range(n - hops, hops + 1)]
        return found

    def home_copy(stage, home, send, recv, source, index):
        return pltpu.make_async_remote_copy(
            src_ref=stage.at[index],
            dst_ref=home.at[me],
            send_sem=send.at[me ^ source],
            recv_sem=recv.at[me ^ source],
            device_id={"expert": source},
            device_id_type=MESH,
        )

    def home_local(stage, home, index):
        return pltpu.make_async_copy(
            stage.at[lax.rem(me, per)], home.at[me], local_s.at[index]
        )

    def go_home(stage, home, send, recv, which, index):
        index = lax.rem(index + 4 * n, n)
        for sub in range(per):
            source = lax.rem(index + group, n) * per + sub

            @pl.when(source != me)
            def _():
                home_copy(stage, home, send, recv, source, index * per + sub).start()

            @pl.when(source == me)
            def _():
                home_local(stage, home, which).start()

    def answer(index):
        at = lax.rem(index + 4 * n, n) * per
        stage_o[pl.ds(at, per)] = blocks(nn(act[0, chunk(index), :], wd[...]))
        go_home(stage_o, home_o, o_s, o_r, 2, index)

    def back(index):
        at = lax.rem(index + 4 * n, n) * per
        stage_b[pl.ds(at, per)] = blocks(
            nt(act[1, chunk(index), :], wg[...]) + nt(act[2, chunk(index), :], wu[...])
        )
        go_home(stage_b, home_b, b_s, b_r, 3, index)

    def pair_copy(u, k):
        return pltpu.make_async_remote_copy(
            src_ref=pair_out.at[u, k],
            dst_ref=pair_in.at[u, k],
            send_sem=pair_s.at[u, k],
            recv_sem=pair_r.at[u, k],
            device_id={"expert": partner},
            device_id_type=MESH,
        )

    def grad_copy(u, k):
        piece = slice(k * third, (k + 1) * third)
        dest = grad_out[u].at[piece, :] if u == 0 else grad_out[u].at[:, piece]
        return pltpu.make_async_copy(grads.at[u, k], dest, grad_s.at[u, k])

    def got_copy(u, k):
        return pltpu.make_async_copy(pair_in.at[u, k], pair_got.at[u, k], got_s.at[u, k])

    def weight_grad(u, k):
        piece = slice(k * third, (k + 1) * third)
        if u == 0:
            value = tn(act[0, :, piece], gb[...])
        else:
            value = tn(xb[...], act[u, :, piece])
        pair_out[u, k] = value.astype(BF16)
        pair_copy(u, k).start()
        grads[u, k] = value
        grad_copy(u, k).start()

    step = 128 if half % 128 == 0 else half

    def activate(sub):
        for col in range(sub * half, (sub + 1) * half, step):
            gate = rs_total(0, col, step)
            up = rs_total(1, col, step)
            own_gu[:, col : col + step] = gate
            own_gu[:, hidden + col : hidden + col + step] = up
            act[0, chunk(z), col : col + step] = (gate * jax.nn.sigmoid(gate) * up).astype(BF16)

    def activate_grads(sub):
        for col in range(sub * half, (sub + 1) * half, step):
            gate = own_gu[:, col : col + step]
            up = own_gu[:, hidden + col : hidden + col + step]
            grad = rs_total(2 + sub, col - sub * half, step)
            sigma = jax.nn.sigmoid(gate)
            act[1, chunk(z), col : col + step] = (
                grad * up * sigma * (1.0 + gate * (1.0 - sigma))
            ).astype(BF16)
            act[2, chunk(z), col : col + step] = (grad * (gate * sigma)).astype(BF16)

    for way in range(2):
        for t in range(2):
            rs_send(t, way, 0)

    first_d, first_hid = lag, hops
    first_gate = lag + hops
    first_up = first_gate + late
    pending = []
    for slot_id in range(first_up + hops):
        if slot_id < hops:
            for offset in later[slot_id]:
                fill_x(z + offset)
            for t in range(2):
                rs_step(t, slot_id)
                cut = 2 * slot_id + t
                if slot_id < first_d:
                    ahead = order[cut * n // (2 * first_d) : (cut + 1) * n // (2 * first_d)]
                    dispatch(stage_g, land_g, g_s, g_r, 1, ahead)
        s = slot_id - first_d
        if 0 <= s < hops:
            for offset in later[s]:
                fill_g(z + offset)
            for t in range(2, 4):
                rs_step(t, s)
        s = slot_id - first_hid
        if 0 <= s < hops:
            ag_step(0, s)
            for index in arrived(s):
                answer(index)
            if s == hops - 1:
                pending += [(0, k) for k in range(3)]
        s = slot_id - first_gate
        if 0 <= s < hops:
            ag_step(1, s)
            if s == hops - 1:
                pending += [(1, k) for k in range(3)]
        s = slot_id - first_up
        if 0 <= s < hops:
            ag_step(2, s)
            for index in arrived(s):
                back(index)
        if slot_id + 1 == first_d:
            for offset in order[:3]:
                fill_g(z + offset)
            for way in range(2):
                for t in range(2, 4):
                    rs_send(t, way, 0)
        if slot_id + 1 == first_hid:
            for sub in range(2):
                activate(sub)
                ag_first(0, sub)
            answer(z)
        if slot_id + 1 == first_gate:
            for sub in range(2):
                activate_grads(sub)
                ag_first(1, sub)
        if slot_id + 1 == first_up:
            for sub in range(2):
                ag_first(2, sub)
            back(z)
        for item in pending:
            weight_grad(*item)
        pending = []
    for k in range(3):
        weight_grad(2, k)

    def take_pair(u):
        for k in range(3):
            pair_copy(u, k).wait()
            got_copy(u, k).start()

    take_pair(0)
    @pl.loop(1, n_exp)
    def _(o):
        pltpu.make_async_remote_copy(
            src_ref=stage_o.at[place(me ^ o, me)],
            dst_ref=home_o.at[me ^ o],
            send_sem=o_s.at[o],
            recv_sem=o_r.at[o],
            device_id={"expert": me ^ o},
            device_id_type=MESH,
        ).wait()

    home_local(stage_o, home_o, 2).wait()
    got = flat(home_o[...])
    y[...] = (tn(high[...], got) + tn(low[...], got)).astype(BF16)

    @pl.loop(1, n_exp)
    def _(o):
        pltpu.make_async_remote_copy(
            src_ref=stage_b.at[place(me ^ o, me)],
            dst_ref=home_b.at[me ^ o],
            send_sem=b_s.at[o],
            recv_sem=b_r.at[o],
            device_id={"expert": me ^ o},
            device_id_type=MESH,
        ).wait()

    home_local(stage_b, home_b, 3).wait()
    gt[...] = tn(sel[...], flat(home_b[...])).astype(BF16)

    for u in range(1, 3):
        take_pair(u)
    for u in range(3):
        for k in range(3):
            grad_copy(u, k).wait()
            got_copy(u, k).wait()

    for copy in started:
        copy.wait_send()

    @pl.loop(1, n_exp)
    def _(o):
        dispatch_copy(stage_x, land_x, x_s, x_r, me ^ o, me).wait_send()
        dispatch_copy(stage_g, land_g, g_s, g_r, me ^ o, me).wait_send()


def finish(
    paired,
    y_in,
    gt_in,
    gd_in,
    gg_in,
    gu_in,
    other,
    y,
    gt,
    gd,
    gg,
    gu,
    small,
    sum_d,
    sum_g,
    sum_u,
    got,
    s_in,
    s_out,
    s_pass,
):
    third = other.shape[2]
    keep = paired[...].astype(F32)
    arrays = ((gd_in, sum_d, gd), (gg_in, sum_g, gg), (gu_in, sum_u, gu))
    loads = []
    for u, (src, mine, _) in enumerate(arrays):
        both = (
            pltpu.make_async_copy(other.at[u], got.at[u], s_in.at[u, 0]),
            pltpu.make_async_copy(src, mine, s_in.at[u, 1]),
        )
        for load in both:
            load.start()
        loads.append(both)
    passed = []
    for k, ref in enumerate((y_in, gt_in)):
        load = pltpu.make_async_copy(ref, small.at[k], s_pass.at[0, k])
        load.start()
        passed.append(load)
    stores = []
    for k, ref in enumerate((y, gt)):
        passed[k].wait()
        store = pltpu.make_async_copy(small.at[k], ref, s_pass.at[1, k])
        store.start()
        stores.append(store)
    for u, (_, mine, dst) in enumerate(arrays):
        for load in loads[u]:
            load.wait()
        for k in range(3):
            piece = slice(k * third, (k + 1) * third)
            value = keep * got[u, k].astype(F32)
            if u == 0:
                mine[piece, :] = mine[piece, :] + value
            else:
                mine[:, piece] = mine[:, piece] + value
        store = pltpu.make_async_copy(mine, dst, s_out.at[u])
        store.start()
        stores.append(store)
    for store in stores:
        store.wait()


def layer_call(sizes, *refs):
    refs = list(refs)
    layer(*sizes, *refs[:9], tuple(refs[9:12]), *refs[12:])


def per_device(tokens, routing, gate_probs, paired, w_gate, w_up, w_down, cotangent):
    n_exp = lax.axis_size("expert")
    n = lax.axis_size("dp")
    count, top = routing.shape
    width = tokens.shape[1]
    hidden = w_gate.shape[2]
    cap = max(2, 5 * count * top // (4 * n_exp))
    rows = n_exp * cap
    own = rows // n
    half = hidden // 2
    third = hidden // 3
    hops = n // 2
    vmem = pl.BlockSpec(memory_space=pltpu.VMEM)
    hbm = pl.BlockSpec(memory_space=pl.ANY)
    dma = pltpu.SemaphoreType.DMA
    lag = min(4, max(hops - 1, 1))
    outs = pl.pallas_call(
        functools.partial(layer_call, (n, n_exp, cap, lag, LATE)),
        out_shape=(
            jax.ShapeDtypeStruct((count, width), BF16),
            jax.ShapeDtypeStruct((count, width), BF16),
            jax.ShapeDtypeStruct((hidden, width), F32),
            jax.ShapeDtypeStruct((width, hidden), F32),
            jax.ShapeDtypeStruct((width, hidden), F32),
            jax.ShapeDtypeStruct((3, 3, third, width), BF16),
        ),
        in_specs=[vmem] * 4 + [hbm] * 3,
        out_specs=(vmem, vmem, hbm, hbm, hbm, hbm),
        scratch_shapes=[
            pltpu.VMEM((width, hidden), BF16),
            pltpu.VMEM((width, hidden), BF16),
            pltpu.VMEM((hidden, width), BF16),
            pltpu.VMEM((rows, count), BF16),
            pltpu.VMEM((rows, count), BF16),
            pltpu.VMEM((rows, count), BF16),
            pltpu.VMEM((rows, 1), F32),
            pltpu.VMEM((n_exp, cap, width), BF16),
            pltpu.VMEM((n_exp, cap, width), BF16),
            pltpu.VMEM((n_exp, cap, width), BF16),
            pltpu.VMEM((n_exp, cap, width), BF16),
            pltpu.VMEM((rows, width), BF16),
            pltpu.VMEM((rows, width), BF16),
            pltpu.VMEM((rows, 2 * hidden), BF16),
            pltpu.VMEM((rows, hidden), BF16),
            pltpu.VMEM((2, 2, hops, own, hidden), BF16),
            pltpu.VMEM((2, 2, hops, own, half), BF16),
            pltpu.VMEM((own, 2 * hidden), F32),
            pltpu.VMEM((3, rows, hidden), BF16),
            pltpu.VMEM((n_exp, cap, width), BF16),
            pltpu.VMEM((n_exp, cap, width), BF16),
            pltpu.VMEM((n_exp, cap, width), BF16),
            pltpu.VMEM((n_exp, cap, width), BF16),
            pltpu.VMEM((3, 3, third, width), F32),
            pltpu.VMEM((3, 3, third, width), BF16),
            pltpu.VMEM((3, 3, third, width), BF16),
            dma((n_exp,)),
            dma((n_exp,)),
            dma((n_exp,)),
            dma((n_exp,)),
            dma((n_exp,)),
            dma((n_exp,)),
            dma((n_exp,)),
            dma((n_exp,)),
            dma((4,)),
            dma((4, 2, hops)),
            dma((4, 2, hops)),
            dma((3, 2, 2, hops)),
            dma((3, 2, 2, hops)),
            dma((3, 3)),
            dma((3, 3)),
            dma((3,)),
            dma((3, 3)),
            dma((3, 3)),
        ],
        compiler_params=pltpu.CompilerParams(
            collective_id=0, has_side_effects=True, vmem_limit_bytes=56 * 1024 * 1024
        ),
    )(
        routing.T,
        gate_probs.T,
        tokens,
        cotangent,
        w_gate[0],
        w_up[0],
        w_down[0],
    )
    y, gt, gd, gg, gu = pl.pallas_call(
        finish,
        out_shape=(
            jax.ShapeDtypeStruct((count, width), BF16),
            jax.ShapeDtypeStruct((count, width), BF16),
            jax.ShapeDtypeStruct((hidden, width), F32),
            jax.ShapeDtypeStruct((width, hidden), F32),
            jax.ShapeDtypeStruct((width, hidden), F32),
        ),
        in_specs=[vmem] + [hbm] * 6,
        out_specs=(hbm,) * 5,
        scratch_shapes=[
            pltpu.VMEM((2, count, width), BF16),
            pltpu.VMEM((hidden, width), F32),
            pltpu.VMEM((width, hidden), F32),
            pltpu.VMEM((width, hidden), F32),
            pltpu.VMEM((3, 3, third, width), BF16),
            dma((3, 2)),
            dma((3,)),
            dma((2, 2)),
        ],
        compiler_params=pltpu.CompilerParams(vmem_limit_bytes=58 * 1024 * 1024),
    )(paired.reshape(1, 1), *outs)
    return y, gt, gg[None], gu[None], gd[None]


def solution(mesh):
    return jax.shard_map(
        per_device,
        mesh=mesh,
        in_specs=(
            P("expert", "dp"),
            P("expert", None),
            P("expert", None),
            P("expert"),
            P("expert", "dp", None),
            P("expert", "dp", None),
            P("expert", None, "dp"),
            P("expert", "dp"),
        ),
        out_specs=(
            P("expert", "dp"),
            P("expert", "dp"),
            P("expert", "dp", None),
            P("expert", "dp", None),
            P("expert", None, "dp"),
        ),
        check_vma=False,
    )
```
